1024 devices in a mesh: order: 32 (over x, z_lo), level: 32 (over z_hi, y, core).
Axes of the slice: x: 4, y: 4, z: 32 (z_hi: 4, z_lo: 8; z = z_hi * 8 + z_lo), core: 2. Of those that a mesh axis runs over, the one named last changes fastest.
Arguments:
- spectral: bfloat16 [512, 512, 2, 2, 128], P('order', 'level'), may hold values from -6 to 6
- factors: bfloat16 [512, 128, 128], P('level'), may hold values from -2 to 2
- legendre: bfloat16 [512, 512, 256], P('order'), may hold values from -12 to 12
- sigma: bfloat16 [256, 128, 1536], P('order', 'level'), may hold values from 0.5 to 2
- order_table: int32 [512], replicated, may hold values from 0 to 511, as said below
- degree_table: int32 [512], replicated, may hold values from 0 to 511, as said below
Outputs:
- grid: bfloat16 [256, 2, 128, 1536], P('order', None, 'level')
The draws below stay inside these ranges and needn't reach their ends.
Inputs may be any that keep to these rules, and one draw needn't show every extreme that they name: `order_table`: a permutation of 0 to 511. `degree_table`: a permutation of 0 to 511.
All inputs are finite; a program needn't handle non-finite values.
Results may differ from the reference program's by a relative error of at most 0.0062.
Values may be sent and summed in bfloat16 or wider, within the bound.
No kernel may reach another device: no remote copies, remote signals or barrier semaphores. Data moves between devices by JAX's collectives and lax.ppermute only.
A program may use at most 32 MiB of HBM per device.

```python
import math
import jax
import jax.numpy as jnp
from jax import lax

NWAVE = 512
LEV = 128
LON = 1536
LAT = 256
MEMB = 2


def draw_order_table(key, part):
    return jax.random.permutation(jax.random.fold_in(key, 11), NWAVE).astype(jnp.int32)


def draw_degree_table(key, part):
    return jax.random.permutation(jax.random.fold_in(key, 12), NWAVE).astype(jnp.int32)


def draw_factors(key, part):
    degrees = draw_degree_table(key, part).astype(jnp.float32)
    noise = jnp.clip(jax.random.normal(jax.random.fold_in(key, 21), (NWAVE, LEV, LEV), jnp.float32), -6.0, 6.0)
    spread = jnp.exp(jax.random.uniform(jax.random.fold_in(key, 22), (NWAVE,), jnp.float32, jnp.log(0.5), jnp.log(2.0)))
    amplitude = spread / jnp.sqrt(NWAVE * (degrees + 1.0))
    core = 0.6 * jnp.eye(LEV, dtype=jnp.float32)[None] + 0.8 * noise / jnp.sqrt(LEV * 1.0)
    return (amplitude[:, None, None] * core).astype(jnp.bfloat16)


def draw_legendre(key, part):
    sines = jax.random.uniform(jax.random.fold_in(key, 31), (LAT,), jnp.float32, -0.5, 0.5)
    sines = jnp.sort(sines)
    orders = jnp.arange(NWAVE, dtype=jnp.float32)
    steps_k = jnp.arange(1, NWAVE, dtype=jnp.float32)
    growth = jnp.concatenate([jnp.zeros((1,), jnp.float32), jnp.cumsum(jnp.log((2.0 * steps_k + 1.0) / (2.0 * steps_k)))])
    log_start = 0.5 * growth[:, None] + 0.5 * orders[:, None] * jnp.log1p(-sines * sines)[None, :]
    start = jnp.exp(log_start)

    def advance(carry, degree):
        last, before = carry
        nval = degree.astype(jnp.float32)
        denom = jnp.maximum(nval * nval - orders * orders, 1.0)
        upper = jnp.sqrt(jnp.maximum(4.0 * nval * nval - 1.0, 0.0) / denom)
        lower = jnp.sqrt(jnp.maximum((nval - 1.0) ** 2 - orders * orders, 0.0) / jnp.maximum(4.0 * (nval - 1.0) ** 2 - 1.0, 1.0))
        recurse = upper[:, None] * (sines[None, :] * last - lower[:, None] * before)
        value = jnp.where(nval < orders[:, None], 0.0, jnp.where(nval == orders[:, None], start, recurse))
        return ((value, last), value)
    zeros = jnp.zeros((NWAVE, LAT), jnp.float32)
    unused, values = lax.scan(advance, (zeros, zeros), jnp.arange(NWAVE, dtype=jnp.int32))
    table = jnp.transpose(values, (1, 0, 2))
    return table[draw_order_table(key, part)].astype(jnp.bfloat16)


def level_of(rng, dims, shards, least, top_value):
    gain, own = 1.0, jax.random.fold_in(rng, 6)
    for axis_at, blocks in shards:
        steps = jnp.exp(jax.random.uniform(jax.random.fold_in(own, axis_at), (blocks,), jnp.float32, least / len(shards), top_value / len(shards)))
        gain = gain * jnp.repeat(steps, dims[axis_at] // blocks).reshape([-1 if axis == axis_at else 1 for axis in range(len(dims))])
    return gain


def gaussian(rng, dims, scale, reach, shards=(), kind=jnp.bfloat16):
    result = scale * jax.random.normal(rng, dims, jnp.float32)
    if shards:
        result = result * level_of(rng, dims, shards, -0.22, 0.18)
    return jnp.clip(result, -reach, reach).astype(kind)


def setup_inputs(seed: int = 0) -> dict:
    keys = jax.random.split(jax.random.key(seed), 7)
    return {
        "spectral": gaussian(keys[0], (NWAVE, NWAVE, MEMB, 2, LEV), 1.0, 6.0, ((0, 32), (1, 32))),
        "factors": draw_factors(jax.random.fold_in(keys[6], 71), 0),
        "legendre": draw_legendre(jax.random.fold_in(keys[6], 71), 0),
        "sigma": jnp.clip(jnp.exp(math.log(2.0) - 1.3862944 * jax.random.uniform(keys[3], (LAT, LEV, LON), jnp.float32) ** level_of(keys[3], (LAT, LEV, LON), ((0, 32), (1, 32)), -0.2, 0.2)), 0.5, 2.0).astype(jnp.bfloat16),
        "order_table": draw_order_table(jax.random.fold_in(keys[6], 71), 0),
        "degree_table": draw_degree_table(jax.random.fold_in(keys[6], 71), 0),
    }


def fourier_matrix(order_table):
    points = jnp.arange(LON, dtype=jnp.int32)
    phase_index = (order_table[:, None] * points[None, :]) % LON
    phase = phase_index.astype(jnp.float32) * (2.0 * jnp.pi / LON)
    weight = jnp.where(order_table == 0, 1.0, 2.0).astype(jnp.float32)[:, None]
    return jnp.stack([weight * jnp.cos(phase), -weight * jnp.sin(phase)]).astype(jnp.bfloat16)


def reference(spectral, factors, legendre, sigma, order_table, degree_table):
    inverse = jnp.zeros((NWAVE,), jnp.int32).at[degree_table].set(jnp.arange(NWAVE, dtype=jnp.int32))
    factors_wide = factors.astype(jnp.float32)
    block_orders = 64
    count_blocks = NWAVE // block_orders
    spec_blocks = spectral.reshape((count_blocks, block_orders) + spectral.shape[1:])
    order_blocks = order_table.reshape(count_blocks, block_orders)
    leg_blocks = legendre.reshape((count_blocks, block_orders) + legendre.shape[1:])

    def synth_block(inputs):
        spec_part, orders_part, leg_part = inputs
        usable = degree_table[None, :] >= orders_part[:, None]
        masked = jnp.where(usable[:, :, None, None, None], spec_part, jnp.zeros((), jnp.bfloat16))
        vertical = jnp.einsum('mnkrl,nql->mnkrq', masked.astype(jnp.float32), factors_wide).astype(jnp.bfloat16)
        coeffs = vertical[:, inverse]
        return jnp.einsum('mnkrq,mnl->lkrqm', coeffs.astype(jnp.float32), leg_part.astype(jnp.float32)).astype(jnp.bfloat16)

    parts = lax.map(synth_block, (spec_blocks, order_blocks, leg_blocks))
    fields = jnp.moveaxis(parts, 0, 4)
    fields = fields.reshape(fields.shape[:4] + (NWAVE,))
    fourier = fourier_matrix(order_table).astype(jnp.float32)
    block_lats = 32
    lat_blocks = LAT // block_lats
    field_blocks = fields.reshape((lat_blocks, block_lats) + fields.shape[1:])
    sigma_blocks = sigma.reshape((lat_blocks, block_lats) + sigma.shape[1:])

    def grid_block(inputs):
        field_part, sigma_part = inputs
        summed = jnp.einsum('lkrqm,rmx->lkqx', field_part.astype(jnp.float32), fourier)
        return (summed * sigma_part.astype(jnp.float32)[:, None]).astype(jnp.bfloat16)

    grid = lax.map(grid_block, (field_blocks, sigma_blocks))
    return grid.reshape((LAT,) + grid.shape[2:])
```

```python
import jax
import jax.numpy as jnp
from jax import lax
from jax.experimental import pallas as pl
from jax.experimental.pallas import tpu as pltpu
from jax.sharding import PartitionSpec as P

F32 = jnp.float32
BF16 = jnp.bfloat16
VMEM = pl.BlockSpec(memory_space=pltpu.VMEM)
HBM = pl.BlockSpec(memory_space=pltpu.HBM)


def in_hbm(x):
    return pltpu.with_memory_space_constraint(x, pltpu.HBM)


def params(mib):
    return pltpu.CompilerParams(vmem_limit_bytes=mib * 2**20)


def vertical_kernel(ord_hbm, deg_hbm, spec_hbm, fac_hbm, out_ref, ords, degs, spec, fac, x32, v32, w32, sems):
    orders, degrees, parts = 16, 16, 4
    per = degrees // parts
    copies = [
        pltpu.make_async_copy(spec_hbm, spec, sems.at[0]),
        pltpu.make_async_copy(ord_hbm, ords, sems.at[1]),
        pltpu.make_async_copy(deg_hbm, degs, sems.at[2]),
    ] + [
        pltpu.make_async_copy(
            fac_hbm.at[pl.ds(t * per, per)], fac.at[pl.ds(t * per, per)], sems.at[3 + t]
        )
        for t in range(parts)
    ]
    for copy in copies:
        copy.start()
    first_order = lax.axis_index("order") * orders
    first_degree = lax.axis_index("level") * degrees
    row = lax.broadcasted_iota(jnp.int32, (orders, 128), 0)
    low = lax.broadcasted_iota(jnp.int32, (32, 128), 1) < 64
    for copy in copies[:3]:
        copy.wait()
    x32[...] = spec[...].astype(F32)
    held = jnp.zeros((orders, 128), jnp.int32)
    for i in range(orders):
        held = jnp.where(row == i, ords[first_order + i], held)
    for j in range(degrees):
        if j % per == 0:
            copies[3 + j // per].wait()
        keep = held <= degs[first_degree + j]
        blocks = [
            jnp.where(keep, x32[pl.ds(j * 4 + p, orders, stride=4 * degrees), :], 0.0)
            for p in range(4)
        ]
        xj = jnp.concatenate(blocks + blocks, axis=0).astype(BF16)
        v32[j] = lax.dot_general(
            fac[j], xj, (((1,), (1,)), ((), ())), preferred_element_type=F32
        )
    for j in range(degrees):
        s = [v32[j, pl.ds(q, 32, stride=4), :] for q in range(4)]
        w32[0, pl.ds(j, 32, stride=degrees), :] = jnp.where(low, s[0], s[1])
        w32[1, pl.ds(j, 32, stride=degrees), :] = jnp.where(low, s[2], s[3])
    out_ref[:, 0:128] = w32[0].astype(BF16)
    out_ref[:, 128:256] = w32[1].astype(BF16)


def align_kernel(deg_ref, leg_ref, out_ref, onehot):
    @pl.when(pl.program_id(0) == 0)
    def _():
        degree = lax.broadcasted_iota(jnp.int32, onehot.shape, 0)
        onehot[...] = jnp.where(degree == deg_ref[...], 1.0, 0.0).astype(BF16)

    slots = onehot.shape[1]
    for i in range(leg_ref.shape[0]):
        out_ref[0, :, i * slots : (i + 1) * slots] = lax.dot_general(
            leg_ref[i], onehot[...], (((0,), (0,)), ((), ())), preferred_element_type=F32
        ).astype(BF16)


def table_kernel(ca_ref, sa_ref, cb_ref, sb_ref, out_ref):
    cb, sb = cb_ref[...], sb_ref[...]
    rows = cb.shape[0]
    per = out_ref.shape[2] // 128
    for a in range(out_ref.shape[0] * per):
        ca, sa = ca_ref[:, a : a + 1], sa_ref[:, a : a + 1]
        lanes = slice((a % per) * 128, (a % per + 1) * 128)
        out_ref[a // per, 0:rows, lanes] = (ca * cb - sa * sb).astype(BF16)
        out_ref[a // per, rows : 2 * rows, lanes] = (-(sa * cb + ca * sb)).astype(BF16)


def legendre_kernel(leg_hbm, r_ref, out_ref, leg, sems):
    groups = leg.shape[0]
    copies = [pltpu.make_async_copy(leg_hbm.at[g], leg.at[g], sems.at[g]) for g in range(groups)]
    for copy in copies:
        copy.start()
    lane = lax.broadcasted_iota(jnp.int32, (1, r_ref.shape[1]), 1) % 16
    r = r_ref[...]
    per = 16 // groups
    acc = jnp.zeros(out_ref.shape, F32)
    for g in range(groups):
        mine = [
            r * jnp.where(lane == g * per + i, 1.0, 0.0).astype(BF16) for i in range(per)
        ]
        rows = jnp.concatenate(mine, axis=0)
        copies[g].wait()
        acc += jnp.dot(leg[g], rows, preferred_element_type=F32)
    out_ref[...] = acc.astype(BF16)


def grid_kernel(r_ref, four_hbm, sig_hbm, out_ref, four, sig, lhs32, sems):
    chunks = four.shape[0]
    copies = [pltpu.make_async_copy(four_hbm.at[t], four.at[t], sems.at[t]) for t in range(chunks)]
    copies.append(pltpu.make_async_copy(sig_hbm, sig, sems.at[chunks]))
    for copy in copies:
        copy.start()
    block = lax.broadcasted_iota(jnp.int32, (8, 128), 1) // 16
    for g in range(4):
        for half in range(2):
            v = [
                r_ref[(g * 8 + t) * 8 : (g * 8 + t + 1) * 8, half * 128 : (half + 1) * 128].astype(F32)
                for t in range(8)
            ]
            for s in (1, 2, 4):
                first = (block & s) == 0
                for t in range(8):
                    if t & s:
                        continue
                    a, b = v[t], v[t + s]
                    v[t] = jnp.where(first, a, pltpu.roll(b, s * 16, 1))
                    v[t + s] = jnp.where(first, pltpu.roll(a, 128 - s * 16, 1), b)
            for cl in range(8):
                c = half * 8 + cl
                q, k, r = c // 4, (c // 2) % 2, c % 2
                lhs32[r * 4 + g, pl.ds(k * 4 + q, 8, stride=8), :] = v[cl]
    lhs = jnp.concatenate([lhs32[t].astype(BF16) for t in range(8)], axis=1)
    copies[chunks].wait()
    width = four.shape[2]
    for t in range(chunks):
        copies[t].wait()
        acc = jnp.dot(lhs, four[t], preferred_element_type=F32)
        res = (acc * sig[:, t * width : (t + 1) * width]).astype(BF16)
        for u in range(16):
            out_ref[u // 2, u % 2, :, t * width : (t + 1) * width] = res[u * 4 : (u + 1) * 4, :]


def per_device(spectral, factors, legendre, sigma, order_table, degree_table):
    lats, levs, points = sigma.shape
    waves = order_table.shape[0]
    dma = pltpu.SemaphoreType.DMA
    send = pl.pallas_call(
        vertical_kernel,
        out_shape=jax.ShapeDtypeStruct((512, 256), BF16),
        in_specs=[HBM] * 4,
        out_specs=VMEM,
        scratch_shapes=[
            pltpu.SMEM((waves,), jnp.int32),
            pltpu.SMEM((waves,), jnp.int32),
            pltpu.VMEM((1024, 128), BF16),
            pltpu.VMEM((16, 128, 128), BF16),
            pltpu.VMEM((1024, 128), F32),
            pltpu.VMEM((16, 128, 128), F32),
            pltpu.VMEM((2, 512, 128), F32),
            dma((7,)),
        ],
        compiler_params=params(8),
        name="vertical",
    )(in_hbm(order_table), in_hbm(degree_table), in_hbm(spectral.reshape(1024, 128)), in_hbm(factors))
    got = lax.all_to_all(send, "level", split_axis=0, concat_axis=0, tiled=True)

    per = 4
    aligned = pl.pallas_call(
        align_kernel,
        out_shape=jax.ShapeDtypeStruct((16 // per, 256, per * 512), BF16),
        grid=(16 // per,),
        in_specs=[
            pl.BlockSpec((1, 512), lambda i: (0, 0)),
            pl.BlockSpec((per, 512, 256), lambda i: (i, 0, 0)),
        ],
        out_specs=pl.BlockSpec((1, 256, per * 512), lambda i: (i, 0, 0)),
        scratch_shapes=[pltpu.VMEM((512, 512), BF16)],
        compiler_params=params(16),
        name="align",
    )(degree_table.reshape(1, waves), in_hbm(legendre))

    step = jnp.arange(128, dtype=jnp.int32)[None, :]
    m = order_table[:, None]
    weight = jnp.where(m == 0, 1.0, 2.0).astype(F32)
    phase_b = ((m * step) % points).astype(F32) * (2.0 * jnp.pi / points)
    phase_a = ((m * (step % 12)) % 12).astype(F32) * (2.0 * jnp.pi / 12)
    fourier = pl.pallas_call(
        table_kernel,
        out_shape=jax.ShapeDtypeStruct((3, 2 * waves, points // 3), BF16),
        in_specs=[VMEM] * 4,
        out_specs=VMEM,
        compiler_params=params(8),
        name="table",
    )(jnp.cos(phase_a), jnp.sin(phase_a), weight * jnp.cos(phase_b), weight * jnp.sin(phase_b))
    sig = jnp.broadcast_to(sigma.astype(F32)[:, None], (lats, 2, levs, points)).reshape(64, points)
    got, aligned, fourier, sig = lax.optimization_barrier((got, aligned, fourier, sig))

    fields = pl.pallas_call(
        legendre_kernel,
        out_shape=jax.ShapeDtypeStruct((256, 256), BF16),
        in_specs=[HBM, VMEM],
        out_specs=VMEM,
        scratch_shapes=[pltpu.VMEM((4, 256, 2048), BF16), dma((4,))],
        compiler_params=params(8),
        name="legendre",
    )(in_hbm(aligned), got)
    got2 = lax.all_to_all(fields, "order", split_axis=0, concat_axis=0, tiled=True)
    return pl.pallas_call(
        grid_kernel,
        out_shape=jax.ShapeDtypeStruct((lats, 2, levs, points), BF16),
        in_specs=[VMEM, HBM, HBM],
        out_specs=VMEM,
        scratch_shapes=[
            pltpu.VMEM((3, 1024, 512), BF16),
            pltpu.VMEM((64, 1536), F32),
            pltpu.VMEM((8, 64, 128), F32),
            dma((4,)),
        ],
        compiler_params=params(8),
        name="grid",
    )(got2, in_hbm(fourier), in_hbm(sig))


def solution(mesh):
    return jax.shard_map(
        per_device,
        mesh=mesh,
        in_specs=(
            P("order", "level", None, None, None),
            P("level", None, None),
            P("order", None, None),
            P("order", "level", None),
            P(),
            P(),
        ),
        out_specs=P("order", None, "level", None),
        check_vma=False,
    )
```

```python
import functools

import jax
import jax.numpy as jnp
from jax import lax
from jax.experimental import pallas as pl
from jax.experimental.pallas import tpu as pltpu
from jax.sharding import PartitionSpec as P

F32 = jnp.float32
BF16 = jnp.bfloat16
VMEM = pl.BlockSpec(memory_space=pltpu.VMEM)
FIRST_LEVEL, FIRST_ORDER = 21, 19
HBM = pl.BlockSpec(memory_space=pltpu.HBM)


def place(first, i):
    return first if i == 0 else 0 if i == first else i


def in_hbm(x):
    return pltpu.with_memory_space_constraint(x, pltpu.HBM)


def in_vmem(x):
    return pltpu.with_memory_space_constraint(x, pltpu.VMEM)


def params(mib):
    return pltpu.CompilerParams(vmem_limit_bytes=mib * 2**20)


def vertical_kernel(ord_hbm, deg_hbm, spec_hbm, fac_hbm, out_ref, ords, degs, spec, fac, x32, v32, w32, sems):
    orders, degrees, parts = 16, 16, 4
    per = degrees // parts
    copies = [
        pltpu.make_async_copy(spec_hbm, spec, sems.at[0]),
        pltpu.make_async_copy(ord_hbm, ords, sems.at[1]),
        pltpu.make_async_copy(deg_hbm, degs, sems.at[2]),
    ] + [
        pltpu.make_async_copy(
            fac_hbm.at[pl.ds(t * per, per)], fac.at[pl.ds(t * per, per)], sems.at[3 + t]
        )
        for t in range(parts)
    ]
    for copy in copies:
        copy.start()
    first_order = lax.axis_index("order") * orders
    first_degree = lax.axis_index("level") * degrees
    row = lax.broadcasted_iota(jnp.int32, (orders, 128), 0)
    low = lax.broadcasted_iota(jnp.int32, (32, 128), 1) < 64
    for copy in copies[:3]:
        copy.wait()
    x32[...] = spec[...].astype(F32)
    held = jnp.zeros((orders, 128), jnp.int32)
    for i in range(orders):
        held = jnp.where(row == i, ords[first_order + i], held)
    for j in range(degrees):
        if j % per == 0:
            copies[3 + j // per].wait()
        keep = held <= degs[first_degree + j]
        blocks = [
            jnp.where(keep, x32[pl.ds(j * 4 + p, orders, stride=4 * degrees), :], 0.0)
            for p in range(4)
        ]
        xj = jnp.concatenate(blocks + blocks, axis=0).astype(BF16)
        v32[j] = lax.dot_general(
            fac[j], xj, (((1,), (1,)), ((), ())), preferred_element_type=F32
        )
    for j in range(degrees):
        s = [v32[j, pl.ds(q, 32, stride=4), :] for q in range(4)]
        w32[0, pl.ds(j, 32, stride=degrees), :] = jnp.where(low, s[0], s[1])
        w32[1, pl.ds(j, 32, stride=degrees), :] = jnp.where(low, s[2], s[3])
    out_ref[:, 0:128] = w32[0].astype(BF16)
    out_ref[:, 128:256] = w32[1].astype(BF16)
    for p in (0, FIRST_LEVEL):
        d = place(FIRST_LEVEL, p) * degrees
        rows = slice(p * degrees, (p + 1) * degrees)
        out_ref[rows, 0:128] = w32[0, d : d + degrees, :].astype(BF16)
        out_ref[rows, 128:256] = w32[1, d : d + degrees, :].astype(BF16)


def align_kernel(kept, deg_ref, leg_ref, near_ref, far_ref, onehot):
    step = pl.program_id(0)

    @pl.when(step == 0)
    def _():
        degree = lax.broadcasted_iota(jnp.int32, onehot.shape, 0)
        a, b = FIRST_LEVEL * 16, FIRST_LEVEL * 16 + 16
        held = jnp.concatenate(
            [deg_ref[:, a:b], deg_ref[:, 16:a], deg_ref[:, 0:16], deg_ref[:, b:]], axis=1
        )
        onehot[...] = jnp.where(degree == held, 1.0, 0.0).astype(BF16)

    for i in range(leg_ref.shape[0]):
        rows = lax.dot_general(
            leg_ref[i], onehot[...], (((0,), (0,)), ((), ())), preferred_element_type=F32
        ).astype(BF16)

        @pl.when(step < kept)
        def _():
            for b in range(4):
                near_ref[step, i * 4 + b] = rows[:, b * 128 : (b + 1) * 128]

        @pl.when(step >= kept)
        def _():
            for b in range(4):
                far_ref[0, i * 4 + b] = rows[:, b * 128 : (b + 1) * 128]


def table_kernel(ca_hbm, sa_hbm, cb_hbm, sb_hbm, out_ref, ca_ref, sa_ref, cb_ref, sb_ref, sems):
    copies = [
        pltpu.make_async_copy(src, dst, sems.at[t])
        for t, (src, dst) in enumerate(
            [(cb_hbm, cb_ref), (sb_hbm, sb_ref), (ca_hbm, ca_ref), (sa_hbm, sa_ref)]
        )
    ]
    for copy in copies:
        copy.start()
    for copy in copies:
        copy.wait()
    cb, sb = cb_ref[...], sb_ref[...]
    rows = cb.shape[0]
    per = out_ref.shape[2] // 128
    for a in range(out_ref.shape[0] * per):
        ca, sa = ca_ref[:, a : a + 1], sa_ref[:, a : a + 1]
        lanes = slice((a % per) * 128, (a % per + 1) * 128)
        out_ref[a // per, 0:rows, lanes] = (ca * cb - sa * sb).astype(BF16)
        out_ref[a // per, rows : 2 * rows, lanes] = (-(sa * cb + ca * sb)).astype(BF16)


def legendre_kernel(near_ref, far_hbm, r_ref, out_ref, far, sems):
    kept, left = near_ref.shape[0], far.shape[0]
    copies = [pltpu.make_async_copy(far_hbm.at[g], far.at[g], sems.at[g]) for g in range(left)]
    for copy in copies:
        copy.start()
    lane = lax.broadcasted_iota(jnp.int32, (1, r_ref.shape[1]), 1) % 16
    r = r_ref[...]
    per = 16 // (kept + left)
    acc = jnp.zeros(out_ref.shape, F32)
    for g in range(kept + left):
        mine = [
            r * jnp.where(lane == g * per + i, 1.0, 0.0).astype(BF16) for i in range(per)
        ]
        rows = jnp.concatenate(mine, axis=0)
        if g >= kept:
            copies[g - kept].wait()
        src, at = (near_ref, g) if g < kept else (far, g - kept)
        leg = jnp.concatenate([src[at, b] for b in range(src.shape[1])], axis=1)
        acc += jnp.dot(leg, rows, preferred_element_type=F32)
    out_ref[...] = acc.astype(BF16)
    for p in (0, FIRST_ORDER):
        d = place(FIRST_ORDER, p) * 8
        out_ref[p * 8 : (p + 1) * 8, :] = acc[d : d + 8, :].astype(BF16)


def grid_kernel(r_ref, four, sig_hbm, out_hbm, sig, res_v, lhs32, sems):
    chunks = four.shape[0]
    copies = []
    fetch = pltpu.make_async_copy(sig_hbm, sig, sems.at[chunks])
    fetch.start()
    block = lax.broadcasted_iota(jnp.int32, (8, 128), 1) // 16
    for g in range(4):
        for half in range(2):
            v = [
                r_ref[p * 8 : (p + 1) * 8, half * 128 : (half + 1) * 128].astype(F32)
                for p in [place(FIRST_ORDER, g * 8 + t) for t in range(8)]
            ]
            for s in (1, 2, 4):
                first = (block & s) == 0
                for t in range(8):
                    if t & s:
                        continue
                    a, b = v[t], v[t + s]
                    v[t] = jnp.where(first, a, pltpu.roll(b, s * 16, 1))
                    v[t + s] = jnp.where(first, pltpu.roll(a, 128 - s * 16, 1), b)
            for cl in range(8):
                c = half * 8 + cl
                q, k, r = c // 4, (c // 2) % 2, c % 2
                lhs32[r * 4 + g, pl.ds(k * 4 + q, 8, stride=8), :] = v[cl]
    lhs = jnp.concatenate([lhs32[t].astype(BF16) for t in range(8)], axis=1)
    width = four.shape[2]
    for t in range(chunks):
        if t == 0:
            fetch.wait()
        acc = jnp.dot(lhs, four[t], preferred_element_type=F32)
        res = (acc * sig[:, t * width : (t + 1) * width].astype(F32)).astype(BF16)
        for u in range(16):
            res_v[u // 2, u % 2, :, t * width : (t + 1) * width] = res[u * 4 : (u + 1) * 4, :]
        lanes = pl.ds(t * width, width)
        copies.append(
            pltpu.make_async_copy(
                res_v.at[:, :, :, lanes], out_hbm.at[:, :, :, lanes], sems.at[t]
            )
        )
        copies[t].start()
    for copy in copies:
        copy.wait()


def per_device(spectral, factors, legendre, sigma, order_table, degree_table):
    lats, levs, points = sigma.shape
    waves = order_table.shape[0]
    dma = pltpu.SemaphoreType.DMA
    send = pl.pallas_call(
        vertical_kernel,
        out_shape=pltpu.VMEM((512, 256), BF16),
        in_specs=[HBM] * 4,
        out_specs=VMEM,
        scratch_shapes=[
            pltpu.SMEM((waves,), jnp.int32),
            pltpu.SMEM((waves,), jnp.int32),
            pltpu.VMEM((1024, 128), BF16),
            pltpu.VMEM((16, 128, 128), BF16),
            pltpu.VMEM((1024, 128), F32),
            pltpu.VMEM((16, 128, 128), F32),
            pltpu.VMEM((2, 512, 128), F32),
            dma((7,)),
        ],
        compiler_params=params(8),
        name="vertical",
    )(in_hbm(order_table), in_hbm(degree_table), in_hbm(spectral.reshape(1024, 128)), in_hbm(factors))
    got = lax.all_to_all(
        send,
        "level",
        split_axis=0,
        concat_axis=0,
        tiled=True,
        axis_index_groups=[[place(FIRST_LEVEL, i) for i in range(32)]],
    )

    per, kept = 2, 5
    groups = 16 // per
    near, far = pl.pallas_call(
        functools.partial(align_kernel, kept),
        out_shape=(
            pltpu.VMEM((kept, per * 4, 256, 128), BF16),
            jax.ShapeDtypeStruct((groups - kept, per * 4, 256, 128), BF16),
        ),
        grid=(groups,),
        in_specs=[
            pl.BlockSpec((1, 512), lambda i: (0, 0)),
            pl.BlockSpec((per, 512, 256), lambda i: (i, 0, 0)),
        ],
        out_specs=(
            VMEM,
            pl.BlockSpec((1, per * 4, 256, 128), lambda i: (jnp.maximum(i - kept, 0), 0, 0, 0)),
        ),
        scratch_shapes=[pltpu.VMEM((512, 512), BF16)],
        compiler_params=params(12),
        name="align",
    )(degree_table.reshape(1, waves), in_hbm(legendre))

    step = jnp.arange(128, dtype=jnp.int32)[None, :]
    m = order_table[:, None]
    weight = jnp.where(m == 0, 1.0, 2.0).astype(F32)
    phase_b = ((m * step) % points).astype(F32) * (2.0 * jnp.pi / points)
    phase_a = ((m * (step % 12)) % 12).astype(F32) * (2.0 * jnp.pi / 12)
    tables = (
        jnp.cos(phase_a),
        jnp.sin(phase_a),
        weight * jnp.cos(phase_b),
        weight * jnp.sin(phase_b),
    )
    sig = jnp.broadcast_to(sigma[:, None], (lats, 2, levs, points)).reshape(64, points)
    got, near, far, tables, sig = lax.optimization_barrier((got, near, far, tables, sig))

    fields = pl.pallas_call(
        legendre_kernel,
        out_shape=pltpu.VMEM((256, 256), BF16),
        in_specs=[VMEM, HBM, VMEM],
        out_specs=VMEM,
        scratch_shapes=[
            pltpu.VMEM((groups - kept, per * 4, 256, 128), BF16),
            dma((groups - kept,)),
        ],
        compiler_params=params(6),
        name="legendre",
    )(in_vmem(near), in_hbm(far), in_vmem(got))
    fields, tables = lax.optimization_barrier((fields, tables))
    fourier = pl.pallas_call(
        table_kernel,
        out_shape=pltpu.VMEM((3, 2 * waves, points // 3), BF16),
        in_specs=[HBM] * 4,
        out_specs=VMEM,
        scratch_shapes=[pltpu.VMEM((waves, 128), F32)] * 4 + [dma((4,))],
        compiler_params=params(4),
        name="table",
    )(*[in_hbm(t) for t in tables])
    got2 = lax.all_to_all(
        fields,
        "order",
        split_axis=0,
        concat_axis=0,
        tiled=True,
        axis_index_groups=[[place(FIRST_ORDER, i) for i in range(32)]],
    )
    return pl.pallas_call(
        grid_kernel,
        out_shape=jax.ShapeDtypeStruct((lats, 2, levs, points), BF16),
        in_specs=[VMEM, VMEM, HBM],
        out_specs=HBM,
        scratch_shapes=[
            pltpu.VMEM((lats * 2 * levs, points), BF16),
            pltpu.VMEM((lats, 2, levs, points), BF16),
            pltpu.VMEM((8, 64, 128), F32),
            dma((4,)),
        ],
        compiler_params=params(4),
        name="grid",
    )(in_vmem(got2), in_vmem(fourier), in_hbm(sig))


def solution(mesh):
    return jax.shard_map(
        per_device,
        mesh=mesh,
        in_specs=(
            P("order", "level", None, None, None),
            P("level", None, None),
            P("order", None, None),
            P("order", "level", None),
            P(),
            P(),
        ),
        out_specs=P("order", None, "level", None),
        check_vma=False,
    )
```

```python
import functools

import jax
import jax.numpy as jnp
from jax import lax
from jax.experimental import pallas as pl
from jax.experimental.pallas import tpu as pltpu
from jax.sharding import PartitionSpec as P

F32 = jnp.float32
BF16 = jnp.bfloat16
VMEM = pl.BlockSpec(memory_space=pltpu.VMEM)
LEVEL_GROUP = (
    21, 0, 1, 2, 6, 3, 7, 4, 5, 8, 24, 9, 25, 10, 14, 26,
    30, 11, 15, 27, 31, 12, 28, 13, 29, 16, 17, 18, 22, 19, 23, 20,
)
ORDER_GROUP = (
    19, 7, 0, 6, 15, 31, 1, 5, 8, 14, 23, 24, 30, 2, 4, 9,
    13, 16, 22, 25, 29, 3, 10, 12, 17, 21, 26, 28, 11, 18, 20, 27,
)
HBM = pl.BlockSpec(memory_space=pltpu.HBM)


def in_hbm(x):
    return pltpu.with_memory_space_constraint(x, pltpu.HBM)


def in_vmem(x):
    return pltpu.with_memory_space_constraint(x, pltpu.VMEM)


def params(mib):
    return pltpu.CompilerParams(vmem_limit_bytes=mib * 2**20)


def vertical_kernel(ord_hbm, deg_hbm, spec_hbm, fac_hbm, out_ref, ords, degs, spec, fac, x32, v32, w32, sems):
    orders, degrees, parts = 16, 16, 4
    per = degrees // parts
    copies = [
        pltpu.make_async_copy(spec_hbm, spec, sems.at[0]),
        pltpu.make_async_copy(ord_hbm, ords, sems.at[1]),
        pltpu.make_async_copy(deg_hbm, degs, sems.at[2]),
    ] + [
        pltpu.make_async_copy(
            fac_hbm.at[pl.ds(t * per, per)], fac.at[pl.ds(t * per, per)], sems.at[3 + t]
        )
        for t in range(parts)
    ]
    for copy in copies:
        copy.start()
    first_order = lax.axis_index("order") * orders
    first_degree = lax.axis_index("level") * degrees
    row = lax.broadcasted_iota(jnp.int32, (orders, 128), 0)
    low = lax.broadcasted_iota(jnp.int32, (32, 128), 1) < 64
    for copy in copies[:3]:
        copy.wait()
    x32[...] = spec[...].astype(F32)
    held = jnp.zeros((orders, 128), jnp.int32)
    for i in range(orders):
        held = jnp.where(row == i, ords[first_order + i], held)
    for j in range(degrees):
        if j % per == 0:
            copies[3 + j // per].wait()
        keep = held <= degs[first_degree + j]
        blocks = [
            jnp.where(keep, x32[pl.ds(j * 4 + p, orders, stride=4 * degrees), :], 0.0)
            for p in range(4)
        ]
        xj = jnp.concatenate(blocks + blocks, axis=0).astype(BF16)
        v32[j] = lax.dot_general(
            fac[j], xj, (((1,), (1,)), ((), ())), preferred_element_type=F32
        )
    for j in range(degrees):
        s = [v32[j, pl.ds(q, 32, stride=4), :] for q in range(4)]
        w32[0, pl.ds(j, 32, stride=degrees), :] = jnp.where(low, s[0], s[1])
        w32[1, pl.ds(j, 32, stride=degrees), :] = jnp.where(low, s[2], s[3])
    for p, d in enumerate(LEVEL_GROUP):
        rows, source = slice(p * degrees, (p + 1) * degrees), slice(d * degrees, (d + 1) * degrees)
        out_ref[rows, 0:128] = w32[0, source, :].astype(BF16)
        out_ref[rows, 128:256] = w32[1, source, :].astype(BF16)


def align_kernel(kept, deg_ref, leg_ref, near_ref, far_ref, onehot):
    step = pl.program_id(0)

    @pl.when(step == 0)
    def _():
        degree = lax.broadcasted_iota(jnp.int32, onehot.shape, 0)
        held = jnp.concatenate([deg_ref[:, d * 16 : (d + 1) * 16] for d in LEVEL_GROUP], axis=1)
        onehot[...] = jnp.where(degree == held, 1.0, 0.0).astype(BF16)

    for i in range(leg_ref.shape[0]):
        rows = lax.dot_general(
            leg_ref[i], onehot[...], (((0,), (0,)), ((), ())), preferred_element_type=F32
        ).astype(BF16)

        @pl.when(step < kept)
        def _():
            for b in range(4):
                near_ref[step, i * 4 + b] = rows[:, b * 128 : (b + 1) * 128]

        @pl.when(step >= kept)
        def _():
            for b in range(4):
                far_ref[0, i * 4 + b] = rows[:, b * 128 : (b + 1) * 128]


def table_kernel(ca_hbm, sa_hbm, cb_hbm, sb_hbm, out_ref, ca_ref, sa_ref, cb_ref, sb_ref, sems):
    copies = [
        pltpu.make_async_copy(src, dst, sems.at[t])
        for t, (src, dst) in enumerate(
            [(cb_hbm, cb_ref), (sb_hbm, sb_ref), (ca_hbm, ca_ref), (sa_hbm, sa_ref)]
        )
    ]
    for copy in copies:
        copy.start()
    for copy in copies:
        copy.wait()
    cb, sb = cb_ref[...], sb_ref[...]
    rows = cb.shape[0]
    per = out_ref.shape[2] // 128
    for a in range(out_ref.shape[0] * per):
        ca, sa = ca_ref[:, a : a + 1], sa_ref[:, a : a + 1]
        lanes = slice((a % per) * 128, (a % per + 1) * 128)
        out_ref[a // per, 0:rows, lanes] = (ca * cb - sa * sb).astype(BF16)
        out_ref[a // per, rows : 2 * rows, lanes] = (-(sa * cb + ca * sb)).astype(BF16)


def legendre_kernel(near_ref, far_hbm, r_ref, out_ref, far, sems):
    kept, left = near_ref.shape[0], far.shape[0]
    copies = [pltpu.make_async_copy(far_hbm.at[g], far.at[g], sems.at[g]) for g in range(left)]
    for copy in copies:
        copy.start()
    lane = lax.broadcasted_iota(jnp.int32, (1, r_ref.shape[1]), 1) % 16
    r = r_ref[...]
    per = 16 // (kept + left)
    acc = jnp.zeros(out_ref.shape, F32)
    for g in range(kept + left):
        mine = [
            r * jnp.where(lane == g * per + i, 1.0, 0.0).astype(BF16) for i in range(per)
        ]
        rows = jnp.concatenate(mine, axis=0)
        if g >= kept:
            copies[g - kept].wait()
        src, at = (near_ref, g) if g < kept else (far, g - kept)
        leg = jnp.concatenate([src[at, b] for b in range(src.shape[1])], axis=1)
        acc += jnp.dot(leg, rows, preferred_element_type=F32)
    for p, d in enumerate(ORDER_GROUP):
        out_ref[p * 8 : (p + 1) * 8, :] = acc[d * 8 : (d + 1) * 8, :].astype(BF16)


def grid_kernel(r_ref, four, sig_hbm, out_hbm, sig, res_v, lhs32, sems):
    chunks = four.shape[0]
    copies = []
    fetch = pltpu.make_async_copy(sig_hbm, sig, sems.at[chunks])
    fetch.start()
    block = lax.broadcasted_iota(jnp.int32, (8, 128), 1) // 16
    for g in range(4):
        for half in range(2):
            v = [
                r_ref[p * 8 : (p + 1) * 8, half * 128 : (half + 1) * 128].astype(F32)
                for p in [ORDER_GROUP.index(g * 8 + t) for t in range(8)]
            ]
            for s in (1, 2, 4):
                first = (block & s) == 0
                for t in range(8):
                    if t & s:
                        continue
                    a, b = v[t], v[t + s]
                    v[t] = jnp.where(first, a, pltpu.roll(b, s * 16, 1))
                    v[t + s] = jnp.where(first, pltpu.roll(a, 128 - s * 16, 1), b)
            for cl in range(8):
                c = half * 8 + cl
                q, k, r = c // 4, (c // 2) % 2, c % 2
                lhs32[r * 4 + g, pl.ds(k * 4 + q, 8, stride=8), :] = v[cl]
    lhs = jnp.concatenate([lhs32[t].astype(BF16) for t in range(8)], axis=1)
    width = four.shape[2]
    for t in range(chunks):
        if t == 0:
            fetch.wait()
        acc = jnp.dot(lhs, four[t], preferred_element_type=F32)
        res = (acc * sig[:, t * width : (t + 1) * width].astype(F32)).astype(BF16)
        for u in range(16):
            res_v[u // 2, u % 2, :, t * width : (t + 1) * width] = res[u * 4 : (u + 1) * 4, :]
        lanes = pl.ds(t * width, width)
        copies.append(
            pltpu.make_async_copy(
                res_v.at[:, :, :, lanes], out_hbm.at[:, :, :, lanes], sems.at[t]
            )
        )
        copies[t].start()
    for copy in copies:
        copy.wait()


def per_device(spectral, factors, legendre, sigma, order_table, degree_table):
    lats, levs, points = sigma.shape
    waves = order_table.shape[0]
    dma = pltpu.SemaphoreType.DMA
    send = pl.pallas_call(
        vertical_kernel,
        out_shape=pltpu.VMEM((512, 256), BF16),
        in_specs=[HBM] * 4,
        out_specs=VMEM,
        scratch_shapes=[
            pltpu.SMEM((waves,), jnp.int32),
            pltpu.SMEM((waves,), jnp.int32),
            pltpu.VMEM((1024, 128), BF16),
            pltpu.VMEM((16, 128, 128), BF16),
            pltpu.VMEM((1024, 128), F32),
            pltpu.VMEM((16, 128, 128), F32),
            pltpu.VMEM((2, 512, 128), F32),
            dma((7,)),
        ],
        compiler_params=params(8),
        name="vertical",
    )(in_hbm(order_table), in_hbm(degree_table), in_hbm(spectral.reshape(1024, 128)), in_hbm(factors))
    got = lax.all_to_all(
        send, "level", split_axis=0, concat_axis=0, tiled=True, axis_index_groups=[LEVEL_GROUP]
    )

    per, kept = 2, 5
    groups = 16 // per
    near, far = pl.pallas_call(
        functools.partial(align_kernel, kept),
        out_shape=(
            pltpu.VMEM((kept, per * 4, 256, 128), BF16),
            jax.ShapeDtypeStruct((groups - kept, per * 4, 256, 128), BF16),
        ),
        grid=(groups,),
        in_specs=[
            pl.BlockSpec((1, 512), lambda i: (0, 0)),
            pl.BlockSpec((per, 512, 256), lambda i: (i, 0, 0)),
        ],
        out_specs=(
            VMEM,
            pl.BlockSpec((1, per * 4, 256, 128), lambda i: (jnp.maximum(i - kept, 0), 0, 0, 0)),
        ),
        scratch_shapes=[pltpu.VMEM((512, 512), BF16)],
        compiler_params=params(12),
        name="align",
    )(degree_table.reshape(1, waves), in_hbm(legendre))

    step = jnp.arange(128, dtype=jnp.int32)[None, :]
    m = order_table[:, None]
    weight = jnp.where(m == 0, 1.0, 2.0).astype(F32)
    phase_b = ((m * step) % points).astype(F32) * (2.0 * jnp.pi / points)
    phase_a = ((m * (step % 12)) % 12).astype(F32) * (2.0 * jnp.pi / 12)
    tables = (
        jnp.cos(phase_a),
        jnp.sin(phase_a),
        weight * jnp.cos(phase_b),
        weight * jnp.sin(phase_b),
    )
    sig = jnp.broadcast_to(sigma[:, None], (lats, 2, levs, points)).reshape(64, points)
    got, near, far, tables, sig = lax.optimization_barrier((got, near, far, tables, sig))

    fields = pl.pallas_call(
        legendre_kernel,
        out_shape=pltpu.VMEM((256, 256), BF16),
        in_specs=[VMEM, HBM, VMEM],
        out_specs=VMEM,
        scratch_shapes=[
            pltpu.VMEM((groups - kept, per * 4, 256, 128), BF16),
            dma((groups - kept,)),
        ],
        compiler_params=params(6),
        name="legendre",
    )(in_vmem(near), in_hbm(far), in_vmem(got))
    fields, tables = lax.optimization_barrier((fields, tables))
    fourier = pl.pallas_call(
        table_kernel,
        out_shape=pltpu.VMEM((3, 2 * waves, points // 3), BF16),
        in_specs=[HBM] * 4,
        out_specs=VMEM,
        scratch_shapes=[pltpu.VMEM((waves, 128), F32)] * 4 + [dma((4,))],
        compiler_params=params(4),
        name="table",
    )(*[in_hbm(t) for t in tables])
    got2 = lax.all_to_all(
        fields, "order", split_axis=0, concat_axis=0, tiled=True, axis_index_groups=[ORDER_GROUP]
    )
    return pl.pallas_call(
        grid_kernel,
        out_shape=jax.ShapeDtypeStruct((lats, 2, levs, points), BF16),
        in_specs=[VMEM, VMEM, HBM],
        out_specs=HBM,
        scratch_shapes=[
            pltpu.VMEM((lats * 2 * levs, points), BF16),
            pltpu.VMEM((lats, 2, levs, points), BF16),
            pltpu.VMEM((8, 64, 128), F32),
            dma((4,)),
        ],
        compiler_params=params(4),
        name="grid",
    )(in_vmem(got2), in_vmem(fourier), in_hbm(sig))


def solution(mesh):
    return jax.shard_map(
        per_device,
        mesh=mesh,
        in_specs=(
            P("order", "level", None, None, None),
            P("level", None, None),
            P("order", None, None),
            P("order", "level", None),
            P(),
            P(),
        ),
        out_specs=P("order", None, "level", None),
        check_vma=False,
    )
```

```python
import functools

import jax
import jax.numpy as jnp
from jax import lax
from jax.experimental import pallas as pl
from jax.experimental.pallas import tpu as pltpu
from jax.sharding import PartitionSpec as P

F32 = jnp.float32
BF16 = jnp.bfloat16
VMEM = pl.BlockSpec(memory_space=pltpu.VMEM)
LEVEL_GROUP = (
    21, 0, 1, 2, 6, 3, 7, 4, 5, 8, 24, 9, 25, 10, 14, 26,
    30, 11, 15, 27, 31, 12, 28, 13, 29, 16, 17, 18, 22, 19, 23, 20,
)
ORDER_GROUP = (
    20, 0, 1, 7, 8, 24, 2, 6, 9, 15, 16, 25, 31, 3, 5, 10,
    14, 17, 23, 26, 30, 4, 11, 13, 18, 22, 27, 29, 12, 19, 21, 28,
)
HBM = pl.BlockSpec(memory_space=pltpu.HBM)


def in_hbm(x):
    return pltpu.with_memory_space_constraint(x, pltpu.HBM)


def in_vmem(x):
    return pltpu.with_memory_space_constraint(x, pltpu.VMEM)


def params(mib):
    return pltpu.CompilerParams(vmem_limit_bytes=mib * 2**20)


def vertical_kernel(ord_hbm, deg_hbm, spec_hbm, fac_hbm, out_ref, ords, degs, spec, fac, x32, v32, w32, sems):
    orders, degrees, parts = 16, 16, 4
    per = degrees // parts
    copies = [
        pltpu.make_async_copy(spec_hbm, spec, sems.at[0]),
        pltpu.make_async_copy(ord_hbm, ords, sems.at[1]),
        pltpu.make_async_copy(deg_hbm, degs, sems.at[2]),
    ] + [
        pltpu.make_async_copy(
            fac_hbm.at[pl.ds(t * per, per)], fac.at[pl.ds(t * per, per)], sems.at[3 + t]
        )
        for t in range(parts)
    ]
    for copy in copies:
        copy.start()
    first_order = lax.axis_index("order") * orders
    first_degree = lax.axis_index("level") * degrees
    row = lax.broadcasted_iota(jnp.int32, (orders, 128), 0)
    low = lax.broadcasted_iota(jnp.int32, (32, 128), 1) < 64
    for copy in copies[:3]:
        copy.wait()
    x32[...] = spec[...].astype(F32)
    held = jnp.zeros((orders, 128), jnp.int32)
    for i in range(orders):
        held = jnp.where(row == i, ords[first_order + i], held)
    for j in range(degrees):
        if j % per == 0:
            copies[3 + j // per].wait()
        keep = held <= degs[first_degree + j]
        blocks = [
            jnp.where(keep, x32[pl.ds(j * 4 + p, orders, stride=4 * degrees), :], 0.0)
            for p in range(4)
        ]
        xj = jnp.concatenate(blocks + blocks, axis=0).astype(BF16)
        v32[j] = lax.dot_general(
            fac[j], xj, (((1,), (1,)), ((), ())), preferred_element_type=F32
        )
    for j in range(degrees):
        s = [v32[j, pl.ds(q, 32, stride=4), :] for q in range(4)]
        w32[0, pl.ds(j, 32, stride=degrees), :] = jnp.where(low, s[0], s[1])
        w32[1, pl.ds(j, 32, stride=degrees), :] = jnp.where(low, s[2], s[3])
    for p, d in enumerate(LEVEL_GROUP):
        rows, source = slice(p * degrees, (p + 1) * degrees), slice(d * degrees, (d + 1) * degrees)
        out_ref[rows, 0:128] = w32[0, source, :].astype(BF16)
        out_ref[rows, 128:256] = w32[1, source, :].astype(BF16)


def align_kernel(kept, deg_ref, leg_ref, near_ref, far_ref, onehot):
    step = pl.program_id(0)

    @pl.when(step == 0)
    def _():
        degree = lax.broadcasted_iota(jnp.int32, onehot.shape, 0)
        held = jnp.concatenate([deg_ref[:, d * 16 : (d + 1) * 16] for d in LEVEL_GROUP], axis=1)
        onehot[...] = jnp.where(degree == held, 1.0, 0.0).astype(BF16)

    for i in range(leg_ref.shape[0]):
        rows = lax.dot_general(
            leg_ref[i], onehot[...], (((0,), (0,)), ((), ())), preferred_element_type=F32
        ).astype(BF16)

        @pl.when(step < kept)
        def _():
            for b in range(4):
                near_ref[step, i * 4 + b] = rows[:, b * 128 : (b + 1) * 128]

        @pl.when(step >= kept)
        def _():
            for b in range(4):
                far_ref[0, i * 4 + b] = rows[:, b * 128 : (b + 1) * 128]


def table_kernel(ca_hbm, sa_hbm, cb_hbm, sb_hbm, out_ref, ca_ref, sa_ref, cb_ref, sb_ref, sems):
    copies = [
        pltpu.make_async_copy(src, dst, sems.at[t])
        for t, (src, dst) in enumerate(
            [(cb_hbm, cb_ref), (sb_hbm, sb_ref), (ca_hbm, ca_ref), (sa_hbm, sa_ref)]
        )
    ]
    for copy in copies:
        copy.start()
    for copy in copies:
        copy.wait()
    cb, sb = cb_ref[...], sb_ref[...]
    rows = cb.shape[0]
    per = out_ref.shape[2] // 128
    for a in range(out_ref.shape[0] * per):
        ca, sa = ca_ref[:, a : a + 1], sa_ref[:, a : a + 1]
        lanes = slice((a % per) * 128, (a % per + 1) * 128)
        out_ref[a // per, 0:rows, lanes] = (ca * cb - sa * sb).astype(BF16)
        out_ref[a // per, rows : 2 * rows, lanes] = (-(sa * cb + ca * sb)).astype(BF16)


def legendre_kernel(near_ref, far_hbm, r_ref, out_ref, far, sems):
    kept, left = near_ref.shape[0], far.shape[0]
    copies = [pltpu.make_async_copy(far_hbm.at[g], far.at[g], sems.at[g]) for g in range(left)]
    for copy in copies:
        copy.start()
    lane = lax.broadcasted_iota(jnp.int32, (1, r_ref.shape[1]), 1) % 16
    r = r_ref[...]
    per = 16 // (kept + left)
    acc = jnp.zeros(out_ref.shape, F32)
    for g in range(kept + left):
        mine = [
            r * jnp.where(lane == g * per + i, 1.0, 0.0).astype(BF16) for i in range(per)
        ]
        rows = jnp.concatenate(mine, axis=0)
        if g >= kept:
            copies[g - kept].wait()
        src, at = (near_ref, g) if g < kept else (far, g - kept)
        leg = jnp.concatenate([src[at, b] for b in range(src.shape[1])], axis=1)
        acc += jnp.dot(leg, rows, preferred_element_type=F32)
    for p, d in enumerate(ORDER_GROUP):
        out_ref[p * 8 : (p + 1) * 8, :] = acc[d * 8 : (d + 1) * 8, :].astype(BF16)


def grid_kernel(r_ref, four, sig_hbm, out_hbm, sig, res_v, lhs32, sems):
    chunks = four.shape[0]
    copies = []
    fetch = pltpu.make_async_copy(sig_hbm, sig, sems.at[chunks])
    fetch.start()
    block = lax.broadcasted_iota(jnp.int32, (8, 128), 1) // 16
    for g in range(4):
        for half in range(2):
            v = [
                r_ref[p * 8 : (p + 1) * 8, half * 128 : (half + 1) * 128].astype(F32)
                for p in [ORDER_GROUP.index(g * 8 + t) for t in range(8)]
            ]
            for s in (1, 2, 4):
                first = (block & s) == 0
                for t in range(8):
                    if t & s:
                        continue
                    a, b = v[t], v[t + s]
                    v[t] = jnp.where(first, a, pltpu.roll(b, s * 16, 1))
                    v[t + s] = jnp.where(first, pltpu.roll(a, 128 - s * 16, 1), b)
            for cl in range(8):
                c = half * 8 + cl
                q, k, r = c // 4, (c // 2) % 2, c % 2
                lhs32[r * 4 + g, pl.ds(k * 4 + q, 8, stride=8), :] = v[cl]
    lhs = jnp.concatenate([lhs32[t].astype(BF16) for t in range(8)], axis=1)
    width = four.shape[2]
    for t in range(chunks):
        if t == 0:
            fetch.wait()
        acc = jnp.dot(lhs, four[t], preferred_element_type=F32)
        res = (acc * sig[:, t * width : (t + 1) * width].astype(F32)).astype(BF16)
        for u in range(16):
            res_v[u // 2, u % 2, :, t * width : (t + 1) * width] = res[u * 4 : (u + 1) * 4, :]
        lanes = pl.ds(t * width, width)
        copies.append(
            pltpu.make_async_copy(
                res_v.at[:, :, :, lanes], out_hbm.at[:, :, :, lanes], sems.at[t]
            )
        )
        copies[t].start()
    for copy in copies:
        copy.wait()


def per_device(spectral, factors, legendre, sigma, order_table, degree_table):
    lats, levs, points = sigma.shape
    waves = order_table.shape[0]
    dma = pltpu.SemaphoreType.DMA
    send = pl.pallas_call(
        vertical_kernel,
        out_shape=pltpu.VMEM((512, 256), BF16),
        in_specs=[HBM] * 4,
        out_specs=VMEM,
        scratch_shapes=[
            pltpu.SMEM((waves,), jnp.int32),
            pltpu.SMEM((waves,), jnp.int32),
            pltpu.VMEM((1024, 128), BF16),
            pltpu.VMEM((16, 128, 128), BF16),
            pltpu.VMEM((1024, 128), F32),
            pltpu.VMEM((16, 128, 128), F32),
            pltpu.VMEM((2, 512, 128), F32),
            dma((7,)),
        ],
        compiler_params=params(8),
        name="vertical",
    )(in_hbm(order_table), in_hbm(degree_table), in_hbm(spectral.reshape(1024, 128)), in_hbm(factors))
    got = lax.all_to_all(
        send, "level", split_axis=0, concat_axis=0, tiled=True, axis_index_groups=[LEVEL_GROUP]
    )

    per, kept = 2, 6
    groups = 16 // per
    near, far = pl.pallas_call(
        functools.partial(align_kernel, kept),
        out_shape=(
            pltpu.VMEM((kept, per * 4, 256, 128), BF16),
            jax.ShapeDtypeStruct((groups - kept, per * 4, 256, 128), BF16),
        ),
        grid=(groups,),
        in_specs=[
            pl.BlockSpec((1, 512), lambda i: (0, 0)),
            pl.BlockSpec((per, 512, 256), lambda i: (i, 0, 0)),
        ],
        out_specs=(
            VMEM,
            pl.BlockSpec((1, per * 4, 256, 128), lambda i: (jnp.maximum(i - kept, 0), 0, 0, 0)),
        ),
        scratch_shapes=[pltpu.VMEM((512, 512), BF16)],
        compiler_params=params(12),
        name="align",
    )(degree_table.reshape(1, waves), in_hbm(legendre))

    step = jnp.arange(128, dtype=jnp.int32)[None, :]
    m = order_table[:, None]
    weight = jnp.where(m == 0, 1.0, 2.0).astype(F32)
    phase_b = ((m * step) % points).astype(F32) * (2.0 * jnp.pi / points)
    phase_a = ((m * (step % 12)) % 12).astype(F32) * (2.0 * jnp.pi / 12)
    tables = (
        jnp.cos(phase_a),
        jnp.sin(phase_a),
        weight * jnp.cos(phase_b),
        weight * jnp.sin(phase_b),
    )
    sig = jnp.broadcast_to(sigma[:, None], (lats, 2, levs, points)).reshape(64, points)
    got, near, far, tables, sig = lax.optimization_barrier((got, near, far, tables, sig))

    fields = pl.pallas_call(
        legendre_kernel,
        out_shape=pltpu.VMEM((256, 256), BF16),
        in_specs=[VMEM, HBM, VMEM],
        out_specs=VMEM,
        scratch_shapes=[
            pltpu.VMEM((groups - kept, per * 4, 256, 128), BF16),
            dma((groups - kept,)),
        ],
        compiler_params=params(6),
        name="legendre",
    )(in_vmem(near), in_hbm(far), in_vmem(got))
    fields, tables = lax.optimization_barrier((fields, tables))
    fourier = pl.pallas_call(
        table_kernel,
        out_shape=pltpu.VMEM((3, 2 * waves, points // 3), BF16),
        in_specs=[HBM] * 4,
        out_specs=VMEM,
        scratch_shapes=[pltpu.VMEM((waves, 128), F32)] * 4 + [dma((4,))],
        compiler_params=params(4),
        name="table",
    )(*[in_hbm(t) for t in tables])
    got2 = lax.all_to_all(
        fields, "order", split_axis=0, concat_axis=0, tiled=True, axis_index_groups=[ORDER_GROUP]
    )
    return pl.pallas_call(
        grid_kernel,
        out_shape=jax.ShapeDtypeStruct((lats, 2, levs, points), BF16),
        in_specs=[VMEM, VMEM, HBM],
        out_specs=HBM,
        scratch_shapes=[
            pltpu.VMEM((lats * 2 * levs, points), BF16),
            pltpu.VMEM((lats, 2, levs, points), BF16),
            pltpu.VMEM((8, 64, 128), F32),
            dma((4,)),
        ],
        compiler_params=params(4),
        name="grid",
    )(in_vmem(got2), in_vmem(fourier), in_hbm(sig))


def solution(mesh):
    return jax.shard_map(
        per_device,
        mesh=mesh,
        in_specs=(
            P("order", "level", None, None, None),
            P("level", None, None),
            P("order", None, None),
            P("order", "level", None),
            P(),
            P(),
        ),
        out_specs=P("order", None, "level", None),
        check_vma=False,
    )
```
